32 devices in a mesh: fsdp: 4 (over z), ctx: 4 (over y, x), tp: 2 (over core).
Axes of the slice: x: 2, y: 2, z: 4, core: 2. Of those that a mesh axis runs over, the one named last changes fastest.
Arguments:
- hidden_in: bfloat16 [4, 8, 512, 1024], P(None, 'fsdp', 'ctx'), may hold values from -6 to 6
- lengths: int32 [4, 8], P(None, 'fsdp'), may hold values from 128 to 512, as said below
- cotangent: bfloat16 [4, 8, 512, 1024], P(None, 'fsdp', 'ctx'), may hold values from -6 to 6
- w_qkv: bfloat16 [1024, 3, 1024], P(('fsdp', 'ctx'), None, 'tp'), may hold values from -0.1875 to 0.1875
- q_bias: bfloat16 [2, 512], P('tp', ('fsdp', 'ctx')), may hold values from -3 to 3
- v_bias: bfloat16 [2, 512], P('tp', ('fsdp', 'ctx')), may hold values from -0.1875 to 0.1875
- w_out: bfloat16 [1024, 1024], P('tp', ('fsdp', 'ctx')), may hold values from -3 to 3
- out_bias: bfloat16 [1024], P(('fsdp', 'ctx')), may hold values from -3 to 3
- norm1_gain: bfloat16 [1024], P(('fsdp', 'ctx')), may hold values from 0.5 to 1.5
- norm1_shift: bfloat16 [1024], P(('fsdp', 'ctx')), may hold values from -3 to 3
- w_up: bfloat16 [1024, 4096], P(('fsdp', 'ctx'), 'tp'), may hold values from -0.1875 to 0.1875
- up_bias: bfloat16 [2, 2048], P('tp', ('fsdp', 'ctx')), may hold values from -3 to 3
- w_down: bfloat16 [4096, 1024], P('tp', ('fsdp', 'ctx')), may hold values from -0.09375 to 0.09375
- down_bias: bfloat16 [1024], P(('fsdp', 'ctx')), may hold values from -3 to 3
- norm2_gain: bfloat16 [1024], P(('fsdp', 'ctx')), may hold values from 0.5 to 1.5
- norm2_shift: bfloat16 [1024], P(('fsdp', 'ctx')), may hold values from -3 to 3
Outputs:
- output: bfloat16 [4, 8, 512, 1024], P(None, 'fsdp', 'ctx')
- input_grad: float32 [4, 8, 512, 1024], P(None, 'fsdp', 'ctx')
- grad_w_qkv: float32 [1024, 3, 1024], P(('fsdp', 'ctx'), None, 'tp')
- grad_q_bias: float32 [2, 512], P('tp', ('fsdp', 'ctx'))
- grad_v_bias: float32 [2, 512], P('tp', ('fsdp', 'ctx'))
- grad_w_out: float32 [1024, 1024], P('tp', ('fsdp', 'ctx'))
- grad_out_bias: float32 [1024], P(('fsdp', 'ctx'))
- grad_norm1_gain: float32 [1024], P(('fsdp', 'ctx'))
- grad_norm1_shift: float32 [1024], P(('fsdp', 'ctx'))
- grad_w_up: float32 [1024, 4096], P(('fsdp', 'ctx'), 'tp')
- grad_up_bias: float32 [2, 2048], P('tp', ('fsdp', 'ctx'))
- grad_w_down: float32 [4096, 1024], P('tp', ('fsdp', 'ctx'))
- grad_down_bias: float32 [1024], P(('fsdp', 'ctx'))
- grad_norm2_gain: float32 [1024], P(('fsdp', 'ctx'))
- grad_norm2_shift: float32 [1024], P(('fsdp', 'ctx'))
The draws below stay inside these ranges and needn't reach their ends.
Inputs may be any that keep to these rules, and one draw needn't show every extreme that they name: The first lengths[m, s] positions of a slot are valid. Some slot has 512 valid positions and some slot 128.
All inputs are finite; a program needn't handle non-finite values.
Results may differ from the reference program's by a relative error of at most 0.014.
Values may be sent and summed in bfloat16 or wider, within the bound.
No kernel may reach another device: no remote copies, remote signals or barrier semaphores. Data moves between devices by JAX's collectives and lax.ppermute only.
A program may use at most 192 MiB of HBM per device.

```python
import jax
import jax.numpy as jnp
from jax import lax

D = 1024
H = 16
DH = 64
FF = 4096
HD = 1024
SEQ = 512
LEN_MIN = 128
MB = 4
SLOTS = 8
N_TP = 2


def draw_lengths(key, part):
    slot_total = MB * SLOTS
    draw_key, long_key, short_key = jax.random.split(key, 3)
    drawn_len = jax.random.randint(draw_key, (slot_total,), LEN_MIN, SEQ + 1)
    long_spot = jax.random.randint(long_key, (), 0, slot_total)
    short_spot = (long_spot + jax.random.randint(short_key, (), 1, slot_total)) % slot_total
    places = jnp.arange(slot_total)
    drawn_len = jnp.where(places == long_spot, SEQ, drawn_len)
    drawn_len = jnp.where(places == short_spot, LEN_MIN, drawn_len)
    return drawn_len.reshape(MB, SLOTS).astype(jnp.int32)


def block_scale(rng, extent, cuts, smallest, high):
    factor_of = 1.0
    for position, blocks in cuts:
        draws = jax.random.uniform(jax.random.fold_in(jax.random.fold_in(rng, 6), position), (blocks,), jnp.float32, smallest / len(cuts), high / len(cuts))
        factor_of = factor_of * jnp.repeat(jnp.exp(draws), extent[position] // blocks).reshape((-1,) + (1,) * (len(extent) - 1 - position))
    return factor_of


def bell_draw(stream_key, extent, spread, reach, shards=(), kind=jnp.bfloat16):
    array = jax.random.normal(stream_key, extent, jnp.float32) * spread
    if len(shards) > 0:
        array = block_scale(stream_key, extent, shards, -0.22, 0.18) * array
    return jnp.clip(array, min=-reach, max=reach).astype(kind)


def setup_inputs(seed: int = 0) -> dict:
    seeds = jax.random.split(jax.random.key(seed), 17)
    return {
        "hidden_in": bell_draw(seeds[0], (MB, SLOTS, SEQ, D), 1.0, 6.0, ((1, 4), (2, 4))),
        "lengths": draw_lengths(jax.random.fold_in(seeds[16], 71), 0),
        "cotangent": bell_draw(seeds[2], (MB, SLOTS, SEQ, D), 1.0, 6.0, ((1, 4), (2, 4))),
        "w_qkv": bell_draw(seeds[3], (D, 3, HD), D ** -0.5, 0.1875, ((0, 16), (2, 2))),
        "q_bias": bell_draw(seeds[4], (N_TP, HD // N_TP), 0.5, 3.0, ((0, 2), (1, 16))),
        "v_bias": bell_draw(seeds[5], (N_TP, HD // N_TP), 0.03, 0.1875, ((0, 2), (1, 16))),
        "w_out": bell_draw(seeds[6], (HD, D), 4 ** -0.5, 3.0, ((0, 2), (1, 16))),
        "out_bias": bell_draw(seeds[7], (D,), 0.5, 3.0, ((0, 16),)),
        "norm1_gain": jnp.clip(1.0 + 0.1 * jax.random.normal(seeds[8], (D,), jnp.float32), 0.5, 1.5).astype(jnp.bfloat16),
        "norm1_shift": bell_draw(seeds[9], (D,), 0.5, 3.0, ((0, 16),)),
        "w_up": bell_draw(seeds[10], (D, FF), D ** -0.5, 0.1875, ((0, 16), (1, 2))),
        "up_bias": bell_draw(seeds[11], (N_TP, FF // N_TP), 0.5, 3.0, ((0, 2), (1, 16))),
        "w_down": bell_draw(seeds[12], (FF, D), FF ** -0.5, 0.09375, ((0, 2), (1, 16))),
        "down_bias": bell_draw(seeds[13], (D,), 0.5, 3.0, ((0, 16),)),
        "norm2_gain": jnp.clip(1.0 + 0.1 * jax.random.normal(seeds[14], (D,), jnp.float32), 0.5, 1.5).astype(jnp.bfloat16),
        "norm2_shift": bell_draw(seeds[15], (D,), 0.5, 3.0, ((0, 16),)),
    }


EPSILON = 1e-05

@jax.custom_vjp
def low(v):
    return lax.optimization_barrier(v.astype(jnp.bfloat16)).astype(jnp.float32)

@jax.custom_vjp
def low_back(v):
    return v

def low_keep(v):
    return (low(v), None)

def low_pass(kept, grad):
    return (grad,)

def back_keep(v):
    return (v, None)

def back_low(kept, grad):
    return (low(grad),)
low.defvjp(low_keep, low_pass)
low_back.defvjp(back_keep, back_low)

def layer_norm(values, norm_gain, norm_shift):
    center = values - lax.optimization_barrier(jnp.mean(values, axis=-1, keepdims=True))
    inverse = lax.rsqrt(lax.optimization_barrier(jnp.mean(center * center, axis=-1, keepdims=True)) + EPSILON)
    return center * inverse * norm_gain + norm_shift

def forward(params, hidden, valid):
    w_qkv, q_bias, v_bias, w_out, out_bias, norm1_gain, norm1_shift, w_up, up_bias, w_down, down_bias, norm2_gain, norm2_shift = params
    highest_prec = lax.Precision.HIGHEST
    groups = hidden.shape[0]
    query_bias = q_bias.reshape(-1)
    bias_rows = jnp.stack([query_bias, jnp.zeros_like(query_bias), v_bias.reshape(-1)])
    mixed = jnp.einsum('gtd,dch->gtch', hidden, w_qkv, precision=highest_prec) + bias_rows
    mixed = low_back(low(mixed))
    head_shape = (groups, SEQ, H, DH)
    queries = mixed[:, :, 0].reshape(head_shape)
    key_heads = mixed[:, :, 1].reshape(head_shape)
    value_heads = mixed[:, :, 2].reshape(head_shape)
    scores = jnp.einsum('gqhe,gkhe->ghqk', queries, key_heads, precision=highest_prec) * DH ** (-0.5)
    scores = jnp.where(valid[:, None, None, :], scores, -1e+30)
    scores = low_back(scores)
    highest = lax.optimization_barrier(jnp.max(scores, axis=-1, keepdims=True))
    exponent = jnp.exp(scores - highest)
    probabilities = low(exponent / lax.optimization_barrier(jnp.sum(exponent, axis=-1, keepdims=True)))
    attended = jnp.einsum('ghqk,gkhe->gqhe', probabilities, value_heads, precision=highest_prec).reshape(groups, SEQ, HD)
    attended = low_back(low(attended))
    projected = low_back(jnp.einsum('gth,hd->gtd', attended, w_out, precision=highest_prec))
    normed = layer_norm(hidden + projected + out_bias, norm1_gain, norm1_shift)
    upward = jnp.einsum('gtd,df->gtf', low(normed), w_up, precision=highest_prec) + up_bias.reshape(-1)
    upward = low_back(upward)
    activated = low(jax.nn.gelu(upward, approximate=False))
    downward = low_back(jnp.einsum('gtf,fd->gtd', activated, w_down, precision=highest_prec))
    return layer_norm(normed + downward + down_bias, norm2_gain, norm2_shift)

def reference(hidden_in, lengths, cotangent, w_qkv, q_bias, v_bias, w_out, out_bias, norm1_gain, norm1_shift, w_up, up_bias, w_down, down_bias, norm2_gain, norm2_shift):
    params = tuple((item.astype(jnp.float32) for item in (w_qkv, q_bias, v_bias, w_out, out_bias, norm1_gain, norm1_shift, w_up, up_bias, w_down, down_bias, norm2_gain, norm2_shift)))
    group_size = 4
    group_total = MB * SLOTS // group_size
    inputs = hidden_in.astype(jnp.float32).reshape(group_total, group_size, SEQ, D)
    cotangent_rows = cotangent.astype(jnp.float32).reshape(group_total, group_size, SEQ, D)
    slot_lengths = lengths.reshape(group_total, group_size).astype(jnp.int32)
    positions = jnp.arange(SEQ, dtype=jnp.int32)

    def accumulate(running, item_data):
        hidden, lengths_here, masked_rows = item_data
        valid = positions[None, :] < lengths_here[:, None]
        result, pull = jax.vjp(lambda weights, values: forward(weights, values, valid), params, hidden)
        weight_grads, hidden_grad = pull(masked_rows * valid[:, :, None].astype(jnp.float32))
        running = jax.tree.map(jnp.add, running, weight_grads)
        return (running, (result.astype(jnp.bfloat16), hidden_grad))
    zeros = tuple((jnp.zeros_like(item) for item in params))
    totals, (results, hidden_grads) = lax.scan(accumulate, zeros, (inputs, slot_lengths, cotangent_rows))
    output = results.reshape(MB, SLOTS, SEQ, D)
    input_grad = hidden_grads.reshape(MB, SLOTS, SEQ, D)
    return (output, input_grad, totals[0], totals[1], totals[2], totals[3], totals[4], totals[5], totals[6], totals[7], totals[8], totals[9], totals[10], totals[11], totals[12])
```

```python
import functools

import jax
import jax.numpy as jnp
from jax import lax
from jax.experimental import pallas as pl
from jax.experimental.pallas import tpu as pltpu
from jax.sharding import PartitionSpec as P

DH = 64
LANES = 128
EPSILON = 1e-05
ROOT_HALF = 0.7071067811865476
INV_ROOT_TAU = 0.3989422804014327
MASKED = -1e30
F32 = jnp.float32
BF16 = jnp.bfloat16


def dot(a, b, ca, cb):
    return lax.dot_general(a, b, (((ca,), (cb,)), ((), ())), preferred_element_type=F32)


def head_probs(q, k, lane_head, h, key_ok, scale):
    q_h = jnp.where(lane_head == h, q, jnp.zeros_like(q))
    scores = jnp.where(key_ok, dot(q_h, k, 1, 1) * scale, MASKED)
    exponent = jnp.exp(scores - jnp.max(scores, axis=-1, keepdims=True))
    return exponent * (1.0 / jnp.sum(exponent, axis=-1, keepdims=True))


def attend_body(len_ref, q_ref, k_ref, v_ref, o_ref):
    q, k, v = q_ref[...], k_ref[...], v_ref[...]
    lane_head = lax.broadcasted_iota(jnp.int32, q.shape, 1) // DH
    key_ok = lax.broadcasted_iota(jnp.int32, (q.shape[0], k.shape[0]), 1) < len_ref[pl.program_id(0)]
    out = jnp.zeros(q.shape, F32)
    for h in range(LANES // DH):
        probs = head_probs(q, k, lane_head, h, key_ok, DH**-0.5)
        out = jnp.where(lane_head == h, dot(probs.astype(BF16), v, 1, 0), out)
    o_ref[...] = out.astype(BF16)


def attend_back_body(len_ref, q_ref, k_ref, v_ref, g_ref, dq_ref, dk_ref, dv_ref):
    q, k, v, g = q_ref[...], k_ref[...], v_ref[...], g_ref[...]
    scale = DH**-0.5
    lane_head = lax.broadcasted_iota(jnp.int32, q.shape, 1) // DH
    key_ok = lax.broadcasted_iota(jnp.int32, (q.shape[0], k.shape[0]), 1) < len_ref[pl.program_id(0)]
    dq = jnp.zeros(q.shape, F32)
    dk = jnp.zeros(q.shape, F32)
    dv = jnp.zeros(q.shape, F32)
    for h in range(LANES // DH):
        probs = head_probs(q, k, lane_head, h, key_ok, scale)
        g_h = jnp.where(lane_head == h, g, jnp.zeros_like(g))
        grad_probs = dot(g_h, v, 1, 1)
        inner = jnp.sum(probs * grad_probs, axis=-1, keepdims=True)
        grad_scores = (probs * (grad_probs - inner)).astype(BF16)
        mine = lane_head == h
        dq = jnp.where(mine, dot(grad_scores, k, 1, 0) * scale, dq)
        dk = jnp.where(mine, dot(grad_scores, q, 0, 0) * scale, dk)
        dv = jnp.where(mine, dot(probs.astype(BF16), g, 0, 0), dv)
    dq_ref[...] = dq.astype(BF16)
    dk_ref[...] = dk.astype(BF16)
    dv_ref[...] = dv.astype(BF16)


def qkv_specs(full_len, pairs):
    return [
        pl.BlockSpec((full_len, LANES), functools.partial(lambda s, j, n, off: (s, j + off), off=pairs * i))
        for i in range(3)
    ]


def attend(slot_lengths, mixed, full_len):
    slots, width = slot_lengths.shape[0], mixed.shape[1] // 3
    pairs = width // LANES
    return pl.pallas_call(
        attend_body,
        out_shape=jax.ShapeDtypeStruct((mixed.shape[0], width), BF16),
        grid_spec=pltpu.PrefetchScalarGridSpec(
            num_scalar_prefetch=1,
            grid=(slots, pairs),
            in_specs=qkv_specs(full_len, pairs),
            out_specs=pl.BlockSpec((full_len, LANES), lambda s, j, n: (s, j)),
        ),
        name="attend",
    )(slot_lengths, mixed, mixed, mixed)


def attend_back(slot_lengths, mixed, grad_att, full_len):
    slots, width = slot_lengths.shape[0], mixed.shape[1] // 3
    pairs = width // LANES
    plain = pl.BlockSpec((full_len, LANES), lambda s, j, n: (s, j))
    return pl.pallas_call(
        attend_back_body,
        out_shape=[jax.ShapeDtypeStruct((mixed.shape[0], width), BF16)] * 3,
        grid_spec=pltpu.PrefetchScalarGridSpec(
            num_scalar_prefetch=1,
            grid=(slots, pairs),
            in_specs=qkv_specs(full_len, pairs) + [plain],
            out_specs=[plain] * 3,
        ),
        name="attend_back",
    )(slot_lengths, mixed, mixed, mixed, grad_att)


def swap_cores(value):
    return lax.ppermute(value, "tp", [(0, 1), (1, 0)])


def swap_ctx(value, bit):
    count = lax.axis_size("ctx")
    return lax.ppermute(value, "ctx", [(i, i ^ bit) for i in range(count)])


def gather_rows(shard):
    rows, n = shard.shape
    half = n // 2
    column = lax.all_gather(shard, "fsdp", axis=0, tiled=False)
    outer = column.shape[0]
    a0, b0 = column[:, :, :half], column[:, :, half:]
    a1 = swap_ctx(a0, 1)
    b2 = swap_ctx(b0, 2)
    a23 = swap_ctx(jnp.stack([a0, a1]), 2)
    b13 = swap_ctx(jnp.stack([b0, b2]), 1)
    mine = lax.axis_index("ctx")
    a_all = jnp.concatenate([jnp.stack([a0, a1]), a23], axis=0)
    b_all = jnp.concatenate([b0[None], b13[:1], b2[None], b13[1:]], axis=0)
    full = jnp.stack(
        [
            jnp.concatenate(
                [
                    lax.dynamic_index_in_dim(a_all, mine ^ i, 0, keepdims=False),
                    lax.dynamic_index_in_dim(b_all, mine ^ i, 0, keepdims=False),
                ],
                axis=-1,
            )
            for i in range(4)
        ],
        axis=1,
    )
    return full.reshape(outer * 4 * rows, n)


def scatter_rows(own, other):
    n = own.shape[1]
    half = n // 2
    outer = lax.axis_size("fsdp")
    rows = own.shape[0] // (outer * 4)
    shape = (outer, 4, rows, n)
    mate = swap_cores(other).reshape(shape)
    own = own.reshape(shape)
    mine = lax.axis_index("ctx")

    def piece(d, s):
        cut = slice(0, half) if s == 0 else slice(half, n)
        a = lax.dynamic_index_in_dim(own, mine ^ d, 1, keepdims=False)[:, :, cut]
        b = lax.dynamic_index_in_dim(mate, mine ^ d, 1, keepdims=False)[:, :, cut]
        return a.astype(F32) + b.astype(F32)

    ra = swap_ctx(jnp.stack([piece(2, 0), piece(3, 0)]).astype(BF16), 2)
    rb = swap_ctx(jnp.stack([piece(1, 1), piece(3, 1)]).astype(BF16), 1)
    ra2 = swap_ctx((piece(1, 0) + ra[1].astype(F32)).astype(BF16), 1)
    rb2 = swap_ctx((piece(2, 1) + rb[1].astype(F32)).astype(BF16), 2)
    a = piece(0, 0) + ra[0].astype(F32) + ra2.astype(F32)
    b = piece(0, 1) + rb[0].astype(F32) + rb2.astype(F32)
    column = jnp.concatenate([a, b], axis=-1).astype(BF16)
    column = column.reshape(outer * rows, n)
    return lax.psum_scatter(column, "fsdp", scatter_dimension=0, tiled=True).astype(F32)


def normalize(values, norm_gain, norm_shift):
    center = values - jnp.mean(values, axis=-1, keepdims=True)
    inverse = lax.rsqrt(jnp.mean(center * center, axis=-1, keepdims=True) + EPSILON)
    unit_rows = center * inverse
    return (unit_rows * norm_gain + norm_shift, unit_rows, inverse)


def normalize_back(incoming, unit_rows, inverse, norm_gain):
    scaled = incoming * norm_gain
    inner = jnp.mean(scaled * unit_rows, axis=-1, keepdims=True)
    result = inverse * (scaled - jnp.mean(scaled, axis=-1, keepdims=True) - unit_rows * inner)
    return (result, jnp.sum(incoming * unit_rows, axis=0), jnp.sum(incoming, axis=0))


def gelu_parts(upward):
    cdf = 0.5 * (1.0 + lax.erf(upward * ROOT_HALF))
    slope = cdf + upward * INV_ROOT_TAU * jnp.exp(-0.5 * upward * upward)
    return (upward * cdf).astype(BF16), slope


def pack_rows(vectors, q_bias, v_bias, up_bias, rows):
    per = vectors[0].shape[-1]
    lines = [jnp.pad(v, ((0, 0), (0, LANES - per))) for v in vectors]
    mixed = jnp.concatenate([q_bias, v_bias], axis=-1)
    lines.append(jnp.pad(mixed, ((0, 0), (0, LANES - mixed.shape[-1]))))
    lines.append(jnp.pad(up_bias, ((0, 0), (0, LANES - up_bias.shape[-1]))))
    packed = jnp.stack(lines, axis=1)
    return jnp.pad(packed, ((0, 0), (0, rows - packed.shape[1]), (0, 0)))


def shards(
    hidden_in,
    lengths,
    cotangent,
    w_qkv,
    q_bias,
    v_bias,
    w_out,
    out_bias,
    norm1_gain,
    norm1_shift,
    w_up,
    up_bias,
    w_down,
    down_bias,
    norm2_gain,
    norm2_shift,
):
    micro_count, seq_count, local_len, width = hidden_in.shape
    ctx_count = lax.axis_size("ctx")
    core_count = lax.axis_size("tp")
    core = lax.axis_index("tp")
    owners = lax.axis_size("fsdp") * ctx_count
    full_len = local_len * ctx_count
    pair_count = micro_count * seq_count
    slots = pair_count // (ctx_count * core_count)
    per_core = pair_count // core_count
    rows = w_qkv.shape[0]
    head_width = w_qkv.shape[2]
    qkv_width = 3 * head_width
    hidden_units = w_up.shape[1]
    q_per, up_per = q_bias.shape[1], up_bias.shape[1]

    def to_slots(value):
        value = value.reshape(pair_count, local_len, width)
        value = lax.dynamic_slice_in_dim(value, core * per_core, per_core, 0)
        value = lax.all_to_all(value, "ctx", split_axis=0, concat_axis=1, tiled=True)
        return value.reshape(slots * full_len, width)

    def to_positions(value):
        value = value.reshape(slots, full_len, width)
        value = lax.all_to_all(value, "ctx", split_axis=1, concat_axis=0, tiled=True)
        mate = swap_cores(value)
        first = jnp.where(core == 0, value, mate)
        second = jnp.where(core == 0, mate, value)
        both = jnp.concatenate([first, second], axis=0)
        return both.reshape(micro_count, seq_count, local_len, width)

    inputs = to_slots(hidden_in)
    slot_first = (core * ctx_count + lax.axis_index("ctx")) * slots
    slot_lengths = lax.dynamic_slice_in_dim(lengths.reshape(pair_count), slot_first, slots, 0)

    small = pack_rows(
        [v[None] for v in (out_bias, norm1_gain, norm1_shift, down_bias, norm2_gain, norm2_shift)],
        q_bias,
        v_bias,
        up_bias,
        rows,
    )[0]
    shard_one = jnp.concatenate([w_qkv.reshape(rows, qkv_width), w_out.T, small], axis=1)
    one = gather_rows(shard_one)
    one = (one, swap_cores(one))
    up_w = gather_rows(w_up)
    up_w = (up_w, swap_cores(up_w))
    down_w = gather_rows(w_down.T)
    down_w = (down_w, swap_cores(down_w))

    qkv_w = [w[:, :qkv_width] for w in one]
    out_w = [w[:, qkv_width : qkv_width + head_width] for w in one]
    packs = [
        w[:, qkv_width + head_width :].reshape(owners, rows, LANES)[:, :8].astype(F32) for w in one
    ]

    def vector(line, w=0, start=0, size=rows):
        return packs[w][:, line, start : start + size].reshape(1, owners * size)

    b_out, gain_one, shift_one, b_down, gain_two, shift_two = [vector(i) for i in range(6)]
    both = range(2)

    mixed = []
    for w in both:
        bias = jnp.concatenate(
            [vector(6, w, 0, q_per), jnp.zeros((1, head_width), F32), vector(6, w, q_per, q_per)],
            axis=1,
        )
        mixed.append((dot(inputs, qkv_w[w], 1, 0) + bias).astype(BF16))
    attended = [attend(slot_lengths, mixed[w], full_len) for w in both]
    projected = dot(attended[0], out_w[0], 1, 1) + dot(attended[1], out_w[1], 1, 1)
    normed, unit_one, inverse_one = normalize(
        inputs.astype(F32) + projected + b_out, gain_one, shift_one
    )
    normed_low = normed.astype(BF16)
    activated, slope = [], []
    for w in both:
        act, slp = gelu_parts(dot(normed_low, up_w[w], 1, 0) + vector(7, w, 0, up_per))
        activated.append(act)
        slope.append(slp)
    downward = dot(activated[0], down_w[0], 1, 1) + dot(activated[1], down_w[1], 1, 1)
    result, unit_two, inverse_two = normalize(normed + downward + b_down, gain_two, shift_two)
    output = to_positions(result.astype(BF16))

    place = lax.broadcasted_iota(jnp.int32, (slots, full_len, 1), 1)
    valid = (place < slot_lengths[:, None, None]).reshape(slots * full_len, 1)
    masked_cot = to_slots(cotangent).astype(F32) * valid.astype(F32)
    grad_two, g_gain_two, g_shift_two = normalize_back(masked_cot, unit_two, inverse_two, gain_two)
    g_down_bias = jnp.sum(grad_two, axis=0)
    grad_two_low = grad_two.astype(BF16)
    d_down = [dot(grad_two_low, activated[w], 0, 0).astype(BF16) for w in both]
    g_down = scatter_rows(*d_down)
    grad_up = [
        (dot(grad_two_low, down_w[w], 1, 0) * slope[w]).astype(BF16) for w in both
    ]
    d_up = [dot(normed_low, grad_up[w], 0, 0).astype(BF16) for w in both]
    g_up = scatter_rows(*d_up)
    grad_normed = grad_two + dot(grad_up[0], up_w[0], 1, 1) + dot(grad_up[1], up_w[1], 1, 1)
    grad_one, g_gain_one, g_shift_one = normalize_back(grad_normed, unit_one, inverse_one, gain_one)
    g_out_bias = jnp.sum(grad_one, axis=0)
    grad_one_low = grad_one.astype(BF16)
    d_one = []
    grad_inputs = grad_one
    for w in both:
        d_out = dot(grad_one_low, attended[w], 0, 0).astype(BF16)
        grad_att = dot(grad_one_low, out_w[w], 1, 0).astype(BF16)
        grad_mixed = jnp.concatenate(attend_back(slot_lengths, mixed[w], grad_att, full_len), axis=1)
        g_mixed = jnp.sum(grad_mixed.astype(F32), axis=0)
        d_qkv = dot(inputs, grad_mixed, 0, 0).astype(BF16)
        grad_inputs = grad_inputs + dot(grad_mixed, qkv_w[w], 1, 1)
        g_up_bias = jnp.sum(grad_up[w].astype(F32), axis=0)
        zero = jnp.zeros_like(g_out_bias)
        lines = [g_out_bias, g_gain_one, g_shift_one, g_down_bias, g_gain_two, g_shift_two]
        lines = [(v if w == 0 else zero).reshape(owners, rows) for v in lines]
        d_small = pack_rows(
            lines,
            g_mixed[:head_width].reshape(owners, q_per),
            g_mixed[2 * head_width :].reshape(owners, q_per),
            g_up_bias.reshape(owners, up_per),
            rows,
        ).reshape(owners * rows, LANES)
        d_one.append(jnp.concatenate([d_qkv, d_out, d_small.astype(BF16)], axis=1))
    g_one = scatter_rows(*d_one)
    input_grad = to_positions(grad_inputs.astype(BF16)).astype(F32)

    tail = g_one[:8, qkv_width + head_width :]
    vectors = tail[:6, :rows]
    vectors = vectors + swap_cores(vectors)
    return (
        output,
        input_grad,
        g_one[:, :qkv_width].reshape(rows, 3, head_width),
        tail[6:7, :q_per],
        tail[6:7, q_per : 2 * q_per],
        g_one[:, qkv_width : qkv_width + head_width].T,
        vectors[0],
        vectors[1],
        vectors[2],
        g_up,
        tail[7:8, :up_per],
        g_down.T,
        vectors[3],
        vectors[4],
        vectors[5],
    )


def solution(mesh):
    owner = ("fsdp", "ctx")
    tokens = P(None, "fsdp", "ctx", None)
    weights = (
        P(owner, None, "tp"),
        P("tp", owner),
        P("tp", owner),
        P("tp", owner),
        P(owner),
        P(owner),
        P(owner),
        P(owner, "tp"),
        P("tp", owner),
        P("tp", owner),
        P(owner),
        P(owner),
        P(owner),
    )
    return jax.shard_map(
        shards,
        mesh=mesh,
        in_specs=(tokens, P(None, "fsdp"), tokens) + weights,
        out_specs=(tokens, tokens) + weights,
        check_vma=False,
    )
```

```python
import functools

import jax
import jax.numpy as jnp
from jax import lax
from jax.experimental import pallas as pl
from jax.experimental.pallas import tpu as pltpu
from jax.sharding import PartitionSpec as P

DH = 64
LANES = 128
EPSILON = 1e-05
ROOT_HALF = 0.7071067811865476
INV_ROOT_TAU = 0.3989422804014327
MASKED = -1e30
F32 = jnp.float32
BF16 = jnp.bfloat16


def dot(a, b, ca, cb):
    return lax.dot_general(a, b, (((ca,), (cb,)), ((), ())), preferred_element_type=F32)


def head_probs(q, k, lane_head, h, key_ok, scale):
    q_h = jnp.where(lane_head == h, q, jnp.zeros_like(q))
    scores = jnp.where(key_ok, dot(q_h, k, 1, 1) * scale, MASKED)
    exponent = jnp.exp(scores - jnp.max(scores, axis=-1, keepdims=True))
    return exponent * (1.0 / jnp.sum(exponent, axis=-1, keepdims=True))


def attend_body(len_ref, q_ref, k_ref, v_ref, o_ref):
    q, k, v = q_ref[...], k_ref[...], v_ref[...]
    lane_head = lax.broadcasted_iota(jnp.int32, q.shape, 1) // DH
    key_ok = lax.broadcasted_iota(jnp.int32, (q.shape[0], k.shape[0]), 1) < len_ref[pl.program_id(0)]
    out = jnp.zeros(q.shape, F32)
    for h in range(LANES // DH):
        probs = head_probs(q, k, lane_head, h, key_ok, DH**-0.5)
        out = jnp.where(lane_head == h, dot(probs.astype(BF16), v, 1, 0), out)
    o_ref[...] = out.astype(BF16)


def attend_back_body(len_ref, q_ref, k_ref, v_ref, g_ref, d_ref, sum_ref):
    q, k, v, g = q_ref[...], k_ref[...], v_ref[...], g_ref[...]
    scale = DH**-0.5
    lane_head = lax.broadcasted_iota(jnp.int32, q.shape, 1) // DH
    key_ok = lax.broadcasted_iota(jnp.int32, (q.shape[0], k.shape[0]), 1) < len_ref[pl.program_id(0)]
    grads = [jnp.zeros(q.shape, F32)] * 3
    for h in range(LANES // DH):
        probs = head_probs(q, k, lane_head, h, key_ok, scale)
        g_h = jnp.where(lane_head == h, g, jnp.zeros_like(g))
        grad_probs = dot(g_h, v, 1, 1)
        inner = jnp.sum(probs * grad_probs, axis=-1, keepdims=True)
        grad_scores = (probs * (grad_probs - inner)).astype(BF16)
        mine = lane_head == h
        new = (
            dot(grad_scores, k, 1, 0) * scale,
            dot(grad_scores, q, 0, 0) * scale,
            dot(probs.astype(BF16), g, 0, 0),
        )
        grads = [jnp.where(mine, n, old) for n, old in zip(new, grads)]
    width = d_ref.shape[1] // 3
    for part, grad in enumerate(grads):
        low = grad.astype(BF16)
        start = pl.multiple_of(part * width + pl.program_id(1) * LANES, LANES)
        d_ref[:, pl.ds(start, LANES)] = low
        sum_ref[0, :, pl.ds(start, LANES)] = jnp.sum(low.astype(F32), axis=0, keepdims=True)


def qkv_specs(full_len, pairs):
    return [
        pl.BlockSpec((full_len, LANES), functools.partial(lambda s, j, n, off: (s, j + off), off=pairs * i))
        for i in range(3)
    ]


def attend(slot_lengths, mixed, full_len):
    slots, width = slot_lengths.shape[0], mixed.shape[1] // 3
    pairs = width // LANES
    return pl.pallas_call(
        attend_body,
        out_shape=jax.ShapeDtypeStruct((mixed.shape[0], width), BF16),
        grid_spec=pltpu.PrefetchScalarGridSpec(
            num_scalar_prefetch=1,
            grid=(slots, pairs),
            in_specs=qkv_specs(full_len, pairs),
            out_specs=pl.BlockSpec((full_len, LANES), lambda s, j, n: (s, j)),
        ),
        name="attend",
    )(slot_lengths, mixed, mixed, mixed)


def attend_back(slot_lengths, mixed, grad_att, full_len):
    slots, width = slot_lengths.shape[0], mixed.shape[1] // 3
    pairs = width // LANES
    plain = pl.BlockSpec((full_len, LANES), lambda s, j, n: (s, j))
    return pl.pallas_call(
        attend_back_body,
        out_shape=[
            jax.ShapeDtypeStruct(mixed.shape, BF16),
            jax.ShapeDtypeStruct((slots, 1, mixed.shape[1]), F32),
        ],
        grid_spec=pltpu.PrefetchScalarGridSpec(
            num_scalar_prefetch=1,
            grid=(slots, pairs),
            in_specs=qkv_specs(full_len, pairs) + [plain],
            out_specs=[
                pl.BlockSpec((full_len, mixed.shape[1]), lambda s, j, n: (s, 0)),
                pl.BlockSpec((1, 1, mixed.shape[1]), lambda s, j, n: (s, 0, 0)),
            ],
        ),
        name="attend_back",
    )(slot_lengths, mixed, mixed, mixed, grad_att)


def swap_cores(value):
    return lax.ppermute(value, "tp", [(0, 1), (1, 0)])


def swap_ctx(value, bit):
    count = lax.axis_size("ctx")
    return lax.ppermute(value, "ctx", [(i, i ^ bit) for i in range(count)])


class Order:
    def __init__(self):
        self.last = None

    def tie(self, *values):
        if self.last is not None:
            values, _ = lax.optimization_barrier((values, self.last))
        return values

    def run(self, fn, *values):
        out = fn(*self.tie(*values))
        self.last = jax.tree.leaves(out)[0]
        return out

    def arrive(self, *values):
        values = self.tie(*values)
        self.last = values
        return values


def column_of(shard):
    return lax.all_gather(shard, "fsdp", axis=0, tiled=False)


def send_first(order, column):
    half = column.shape[-1] // 2
    a, b = order.run(lambda c: (c[:, :, :half], c[:, :, half:]), column)
    return dict(a1=swap_ctx(a, 1), b2=swap_ctx(b, 2), a2=swap_ctx(a, 2), b1=swap_ctx(b, 1))


def send_second(order, got):
    a1, b2 = order.arrive(got["a1"], got["b2"])
    return dict(got, a1=a1, b2=b2, a3=swap_ctx(a1, 2), b3=swap_ctx(b2, 1))


def assemble(order, column, got, parts):
    outer, rows, n = column.shape
    half = n // 2
    starts = [sum(parts[:i]) for i in range(len(parts))]
    moves = []
    for i, (start, size) in enumerate(zip(starts, parts)):
        moves.append((0, 0, start, i, 0, size))
        for d in (1, 2, 3):
            for side, base in ((0, 0), (3, half)):
                lo, hi = max(start, base), min(start + size, base + half)
                if lo < hi:
                    moves.append((d + side, d, lo - base, i, lo - start, hi - lo))

    def body(*refs):
        ins, outs, sems = refs[:7], refs[7:-1], refs[-1]
        mine = lax.axis_index("ctx")
        copies = [
            pltpu.make_async_copy(
                ins[src].at[:, :, pl.ds(src_at, size)],
                outs[dst].at[:, mine ^ d, :, pl.ds(dst_at, size)],
                sems.at[i],
            )
            for i, (src, d, src_at, dst, dst_at, size) in enumerate(moves)
        ]
        for c in copies:
            c.start()
        for c in copies:
            c.wait()

    hbm = pl.BlockSpec(memory_space=pl.ANY)
    call = pl.pallas_call(
        body,
        out_shape=[jax.ShapeDtypeStruct((outer, 4, rows, p), column.dtype) for p in parts],
        in_specs=[hbm] * 7,
        out_specs=[hbm] * len(parts),
        scratch_shapes=[pltpu.SemaphoreType.DMA((len(moves),))],
        name="assemble",
    )
    names = ("a1", "a2", "a3", "b1", "b2", "b3")
    full = order.run(call, column, *[got[k] for k in names])
    return [f.reshape(outer * 4 * rows, f.shape[-1]) for f in full]


def fold_first(order, own, mate):
    count = len(own)
    outer = lax.axis_size("fsdp")
    rows = own[0].shape[0] // (outer * 4)
    n = sum(o.shape[1] for o in own)
    half = n // 2

    def body(*refs):
        ins, (send_a, keep_a, send_b, keep_b) = refs[: 2 * count], refs[2 * count :]
        mine = lax.axis_index("ctx")
        for d in range(4):
            sums = [
                ins[i][0, mine ^ d].astype(F32) + ins[count + i][0, mine ^ d].astype(F32)
                for i in range(count)
            ]
            total = (sums[0] if count == 1 else jnp.concatenate(sums, axis=-1)).astype(BF16)
            (send_a if d // 2 else keep_a)[d % 2, 0] = total[:, :half]
            (send_b if d % 2 else keep_b)[d // 2, 0] = total[:, half:]

    def spec(width):
        return pl.BlockSpec((1, 4, rows, width), lambda f: (f, 0, 0, 0))

    call = pl.pallas_call(
        body,
        out_shape=[jax.ShapeDtypeStruct((2, outer, rows, half), BF16)] * 4,
        grid=(outer,),
        in_specs=[spec(o.shape[1]) for o in own] * 2,
        out_specs=[pl.BlockSpec((2, 1, rows, half), lambda f: (0, f, 0, 0))] * 4,
        name="fold_first",
    )
    shaped = [v.reshape(outer, 4, rows, v.shape[1]) for v in (*own, *mate)]
    send_a, keep_a, send_b, keep_b = order.run(call, *shaped)
    return dict(keep_a=keep_a, keep_b=keep_b, a=swap_ctx(send_a, 2), b=swap_ctx(send_b, 1))


def fold_second(order, state):
    _, outer, rows, half = state["keep_a"].shape
    spec = pl.BlockSpec((1, 1, rows, half), lambda f: (1, f, 0, 0))
    out = pl.BlockSpec((1, rows, half), lambda f: (f, 0, 0))

    def body(keep_a, keep_b, a, b, out_a, out_b):
        out_a[0] = (keep_a[0, 0].astype(F32) + a[0, 0].astype(F32)).astype(BF16)
        out_b[0] = (keep_b[0, 0].astype(F32) + b[0, 0].astype(F32)).astype(BF16)

    call = pl.pallas_call(
        body,
        out_shape=[jax.ShapeDtypeStruct((outer, rows, half), BF16)] * 2,
        grid=(outer,),
        in_specs=[spec] * 4,
        out_specs=[out] * 2,
        name="fold_second",
    )
    a, b = order.run(call, *[state[k] for k in ("keep_a", "keep_b", "a", "b")])
    return dict(state, a2=swap_ctx(a, 1), b2=swap_ctx(b, 2))


def fold_third(order, state):
    _, outer, rows, half = state["keep_a"].shape
    four = pl.BlockSpec((1, 1, rows, half), lambda f: (0, f, 0, 0))
    three = pl.BlockSpec((1, rows, half), lambda f: (f, 0, 0))

    def body(keep_a, keep_b, a, b, a2, b2, out):
        for s, (x, y, z) in enumerate(((keep_a, a, a2), (keep_b, b, b2))):
            total = x[0, 0].astype(F32) + y[0, 0].astype(F32) + z[0].astype(F32)
            out[0, :, s * half : (s + 1) * half] = total.astype(BF16)

    call = pl.pallas_call(
        body,
        out_shape=jax.ShapeDtypeStruct((outer, rows, 2 * half), BF16),
        grid=(outer,),
        in_specs=[four] * 4 + [three] * 2,
        out_specs=pl.BlockSpec((1, rows, 2 * half), lambda f: (f, 0, 0)),
        name="fold_third",
    )
    column = order.run(call, *[state[k] for k in ("keep_a", "keep_b", "a", "b", "a2", "b2")])
    column = column.reshape(outer * rows, 2 * half)
    return lax.psum_scatter(column, "fsdp", scatter_dimension=0, tiled=True)


def normalize(values, norm_gain, norm_shift):
    center = values - jnp.mean(values, axis=-1, keepdims=True)
    inverse = lax.rsqrt(jnp.mean(center * center, axis=-1, keepdims=True) + EPSILON)
    unit_rows = center * inverse
    return (unit_rows * norm_gain + norm_shift, unit_rows, inverse)


def normalize_back(incoming, unit_rows, inverse, norm_gain):
    scaled = incoming * norm_gain
    inner = jnp.mean(scaled * unit_rows, axis=-1, keepdims=True)
    result = inverse * (scaled - jnp.mean(scaled, axis=-1, keepdims=True) - unit_rows * inner)
    return (result, jnp.sum(incoming * unit_rows, axis=0), jnp.sum(incoming, axis=0))


def gelu_parts(upward):
    cdf = 0.5 * (1.0 + lax.erf(upward * ROOT_HALF))
    slope = cdf + upward * INV_ROOT_TAU * jnp.exp(-0.5 * upward * upward)
    return (upward * cdf).astype(BF16), slope


def pack_rows(vectors, q_bias, v_bias, up_bias, rows):
    per = vectors[0].shape[-1]
    lines = [jnp.pad(v, ((0, 0), (0, LANES - per))) for v in vectors]
    mixed = jnp.concatenate([q_bias, v_bias], axis=-1)
    lines.append(jnp.pad(mixed, ((0, 0), (0, LANES - mixed.shape[-1]))))
    lines.append(jnp.pad(up_bias, ((0, 0), (0, LANES - up_bias.shape[-1]))))
    packed = jnp.stack(lines, axis=1)
    return jnp.pad(packed, ((0, 0), (0, rows - packed.shape[1]), (0, 0)))


def shards(
    hidden_in,
    lengths,
    cotangent,
    w_qkv,
    q_bias,
    v_bias,
    w_out,
    out_bias,
    norm1_gain,
    norm1_shift,
    w_up,
    up_bias,
    w_down,
    down_bias,
    norm2_gain,
    norm2_shift,
):
    micro_count, seq_count, local_len, width = hidden_in.shape
    ctx_count = lax.axis_size("ctx")
    core_count = lax.axis_size("tp")
    core = lax.axis_index("tp")
    owners = lax.axis_size("fsdp") * ctx_count
    full_len = local_len * ctx_count
    pair_count = micro_count * seq_count
    slots = pair_count // (ctx_count * core_count)
    per_core = pair_count // core_count
    rows = w_qkv.shape[0]
    head_width = w_qkv.shape[2]
    qkv_width = 3 * head_width
    hidden_units = w_up.shape[1]
    q_per, up_per = q_bias.shape[1], up_bias.shape[1]

    def to_slots(value):
        value = value.reshape(pair_count, local_len, width)
        value = lax.dynamic_slice_in_dim(value, core * per_core, per_core, 0)
        value = value.reshape(ctx_count, slots, local_len, width)
        value = lax.all_to_all(value, "ctx", split_axis=0, concat_axis=0, tiled=True)
        return jnp.swapaxes(value, 0, 1).reshape(slots * full_len, width)

    def to_positions(value):
        value = jnp.swapaxes(value.reshape(slots, ctx_count, local_len, width), 0, 1)
        value = lax.all_to_all(value, "ctx", split_axis=0, concat_axis=0, tiled=True)
        return value.reshape(per_core, local_len, width)

    def all_pairs(value, mate):
        first = jnp.where(core == 0, value, mate)
        second = jnp.where(core == 0, mate, value)
        both = jnp.concatenate([first, second], axis=0)
        return both.reshape(micro_count, seq_count, local_len, width)

    order = Order()
    run = order.run
    both = range(2)
    slot_first = (core * ctx_count + lax.axis_index("ctx")) * slots
    slot_lengths = lax.dynamic_slice_in_dim(lengths.reshape(pair_count), slot_first, slots, 0)

    small_width = 2 * LANES
    small = pack_rows(
        [v[None] for v in (out_bias, norm1_gain, norm1_shift, down_bias, norm2_gain, norm2_shift)],
        q_bias,
        v_bias,
        up_bias,
        rows,
    )[0]
    shard_one = jnp.concatenate(
        [w_qkv.reshape(rows, qkv_width), w_out.T, jnp.pad(small, ((0, 0), (0, small_width - LANES)))],
        axis=1,
    )
    column_one = column_of(shard_one)
    column_up = column_of(w_up)
    column_down = column_of(w_down.T)
    inputs = to_slots(hidden_in)
    cot_rows = to_slots(cotangent)

    got_one = send_second(order, send_first(order, column_one))
    got_up = send_first(order, column_up)
    one = assemble(order, column_one, got_one, (qkv_width, head_width, small_width))
    one_mate = [swap_cores(w) for w in one]
    qkv_w, out_w, packed = zip(one, one_mate)
    packs = [p.reshape(owners, rows, small_width)[:, :8, :LANES].astype(F32) for p in packed]

    def vector(line, w=0, start=0, size=rows):
        return packs[w][:, line, start : start + size].reshape(1, owners * size)

    b_out, gain_one, shift_one, b_down, gain_two, shift_two = [vector(i) for i in range(6)]

    def mix(w):
        bias = jnp.concatenate(
            [vector(6, w, 0, q_per), jnp.zeros((1, head_width), F32), vector(6, w, q_per, q_per)],
            axis=1,
        )
        return run(lambda x, k: (dot(x, k, 1, 0) + bias).astype(BF16), inputs, qkv_w[w])

    mixed, attended = [None, None], [None, None]
    mixed[0] = mix(0)
    attended[0] = run(lambda m: attend(slot_lengths, m, full_len), mixed[0])
    got_up = send_second(order, got_up)
    got_down = send_first(order, column_down)
    mixed[1] = mix(1)
    attended[1] = run(lambda m: attend(slot_lengths, m, full_len), mixed[1])
    up_own = assemble(order, column_up, got_up, (hidden_units,))[0]
    up_w = (up_own, swap_cores(up_own))
    projected = run(
        lambda a, b: dot(a, out_w[0], 1, 1) + dot(b, out_w[1], 1, 1), attended[0], attended[1]
    )
    normed, unit_one, inverse_one = normalize(
        inputs.astype(F32) + projected + b_out, gain_one, shift_one
    )
    normed_low = run(lambda n: n.astype(BF16), normed)
    got_down = send_second(order, got_down)
    activated, slope = [], []
    for w in both:
        bias = vector(7, w, 0, up_per)
        act, slp = run(lambda n, k: gelu_parts(dot(n, k, 1, 0) + bias), normed_low, up_w[w])
        activated.append(act)
        slope.append(slp)
    down_own = assemble(order, column_down, got_down, (hidden_units,))[0]
    down_w = (down_own, swap_cores(down_own))
    downward = run(lambda a, k: dot(a, k, 1, 1), activated[0], down_w[0])
    downward = run(lambda a, k, d: d + dot(a, k, 1, 1), activated[1], down_w[1], downward)
    result, unit_two, inverse_two = normalize(normed + downward + b_down, gain_two, shift_two)

    place = lax.broadcasted_iota(jnp.int32, (slots, full_len, 1), 1)
    valid = (place < slot_lengths[:, None, None]).reshape(slots * full_len, 1)
    masked_cot = cot_rows.astype(F32) * valid.astype(F32)
    grad_two, g_gain_two, g_shift_two = normalize_back(masked_cot, unit_two, inverse_two, gain_two)
    g_down_bias = jnp.sum(grad_two, axis=0)
    grad_two_low = run(lambda g: g.astype(BF16), grad_two)
    d_down = [None, None]
    d_down[1] = run(lambda g, a: dot(g, a, 0, 0).astype(BF16), grad_two_low, activated[1])
    mate_down = swap_cores(d_down[1])
    out_slots = to_positions(order.tie(result.astype(BF16))[0])
    d_down[0] = run(lambda g, a: dot(g, a, 0, 0).astype(BF16), grad_two_low, activated[0])
    grad_up = [
        run(lambda g, k, s: (dot(g, k, 1, 0) * s).astype(BF16), grad_two_low, down_w[w], slope[w])
        for w in both
    ]
    fold_down = fold_first(order, [d_down[0]], [mate_down])
    d_up = [None, None]
    d_up[1] = run(lambda n, g: dot(n, g, 0, 0).astype(BF16), normed_low, grad_up[1])
    mate_up = swap_cores(d_up[1])
    d_up[0] = run(lambda n, g: dot(n, g, 0, 0).astype(BF16), normed_low, grad_up[0])
    back_up = run(lambda g, k: dot(g, k, 1, 1), grad_up[0], up_w[0])
    back_up = run(lambda g, k, d: d + dot(g, k, 1, 1), grad_up[1], up_w[1], back_up)
    grad_normed = grad_two + back_up
    fold_down = fold_second(order, fold_down)
    fold_up = fold_first(order, [d_up[0]], [mate_up])
    grad_one, g_gain_one, g_shift_one = normalize_back(grad_normed, unit_one, inverse_one, gain_one)
    g_out_bias = jnp.sum(grad_one, axis=0)
    grad_one_low = run(lambda g: g.astype(BF16), grad_one)
    d_out = [
        run(lambda g, a: dot(g, a, 0, 0).astype(BF16), grad_one_low, attended[w]) for w in both
    ]
    grad_mixed, g_mixed = [None, None], [None, None]

    def back(w):
        grad_att = run(lambda g, k: dot(g, k, 1, 0).astype(BF16), grad_one_low, out_w[w])
        grad_mixed[w], sums = run(
            lambda m, g: attend_back(slot_lengths, m, g, full_len), mixed[w], grad_att
        )
        g_mixed[w] = jnp.sum(sums, axis=0)[0]

    back(1)
    column_down = fold_third(order, fold_down)
    back(0)
    fold_up = fold_second(order, fold_up)

    def small_grads(w):
        g_up_bias = jnp.sum(grad_up[w].astype(F32), axis=0)
        zero = jnp.zeros_like(g_out_bias)
        lines = [g_out_bias, g_gain_one, g_shift_one, g_down_bias, g_gain_two, g_shift_two]
        packed = pack_rows(
            [(v if w == 0 else zero).reshape(owners, rows) for v in lines],
            g_mixed[w][:head_width].reshape(owners, q_per),
            g_mixed[w][2 * head_width :].reshape(owners, q_per),
            g_up_bias.reshape(owners, up_per),
            rows,
        ).reshape(owners * rows, LANES)
        return jnp.pad(packed.astype(BF16), ((0, 0), (0, small_width - LANES)))

    d_small = [small_grads(w) for w in both]
    d_qkv = [None, None]
    d_qkv[1] = run(lambda x, g: dot(x, g, 0, 0).astype(BF16), inputs, grad_mixed[1])
    mate_one = [swap_cores(v) for v in (d_qkv[1], d_out[1], d_small[1])]
    d_qkv[0] = run(lambda x, g: dot(x, g, 0, 0).astype(BF16), inputs, grad_mixed[0])
    fold_one = fold_first(order, [d_qkv[0], d_out[0], d_small[0]], mate_one)
    grad_inputs = run(lambda g, k, d: d + dot(g, k, 1, 1), grad_mixed[0], qkv_w[0], grad_one)
    grad_inputs = run(
        lambda g, k, d: (d + dot(g, k, 1, 1)).astype(BF16), grad_mixed[1], qkv_w[1], grad_inputs
    )
    in_slots = to_positions(grad_inputs)
    column_up = fold_third(order, fold_up)
    fold_one = fold_second(order, fold_one)
    column_one = fold_third(order, fold_one)
    output = all_pairs(out_slots, swap_cores(out_slots))
    input_grad = all_pairs(in_slots, swap_cores(in_slots)).astype(F32)
    g_down, g_up, g_one = [c.astype(F32) for c in (column_down, column_up, column_one)]
    tail = g_one[:8, qkv_width + head_width : qkv_width + head_width + LANES]
    vectors = tail[:6, :rows]
    vectors = vectors + swap_cores(vectors)
    return (
        output,
        input_grad,
        g_one[:, :qkv_width].reshape(rows, 3, head_width),
        tail[6:7, :q_per],
        tail[6:7, q_per : 2 * q_per],
        g_one[:, qkv_width : qkv_width + head_width].T,
        vectors[0],
        vectors[1],
        vectors[2],
        g_up,
        tail[7:8, :up_per],
        g_down.T,
        vectors[3],
        vectors[4],
        vectors[5],
    )


def solution(mesh):
    owner = ("fsdp", "ctx")
    tokens = P(None, "fsdp", "ctx", None)
    weights = (
        P(owner, None, "tp"),
        P("tp", owner),
        P("tp", owner),
        P("tp", owner),
        P(owner),
        P(owner),
        P(owner),
        P(owner, "tp"),
        P("tp", owner),
        P("tp", owner),
        P(owner),
        P(owner),
        P(owner),
    )
    return jax.shard_map(
        shards,
        mesh=mesh,
        in_specs=(tokens, P(None, "fsdp"), tokens) + weights,
        out_specs=(tokens, tokens) + weights,
        check_vma=False,
    )
```

```python
import functools

import jax
import jax.numpy as jnp
import numpy as np
from jax import lax
from jax.experimental import pallas as pl
from jax.experimental.pallas import tpu as pltpu
from jax.sharding import PartitionSpec as P

DH = 64
LANES = 128
EPSILON = 1e-05
ROOT_HALF = 0.7071067811865476
INV_ROOT_TAU = 0.3989422804014327
MASKED = -1e30
CTX = 4
DIRECT = 4
F32 = jnp.float32
BF16 = jnp.bfloat16


def dot(a, b, ca, cb):
    return lax.dot_general(a, b, (((ca,), (cb,)), ((), ())), preferred_element_type=F32)


def head_probs(q, k, lane_head, h, key_ok, scale):
    q_h = jnp.where(lane_head == h, q, jnp.zeros_like(q))
    scores = jnp.where(key_ok, dot(q_h, k, 1, 1) * scale, MASKED)
    exponent = jnp.exp(scores - jnp.max(scores, axis=-1, keepdims=True))
    return exponent * (1.0 / jnp.sum(exponent, axis=-1, keepdims=True))


def key_places(full_len, len_ref):
    row = lax.broadcasted_iota(jnp.int32, (1, full_len), 1)
    local = full_len // CTX
    part = row // local
    return (part ^ len_ref[0]) * local + (row - part * local)


def attend_body(len_ref, q_ref, k_ref, v_ref, o_ref):
    q, k, v = q_ref[...], k_ref[...], v_ref[...]
    lane_head = lax.broadcasted_iota(jnp.int32, q.shape, 1) // DH
    key_ok = key_places(k.shape[0], len_ref) < len_ref[1 + pl.program_id(0)]
    out = jnp.zeros(q.shape, F32)
    for h in range(LANES // DH):
        probs = head_probs(q, k, lane_head, h, key_ok, DH**-0.5)
        out = jnp.where(lane_head == h, dot(probs.astype(BF16), v, 1, 0), out)
    o_ref[...] = out.astype(BF16)


def attend_back_body(len_ref, q_ref, k_ref, v_ref, g_ref, d_ref, sum_ref):
    q, k, v, g = q_ref[...], k_ref[...], v_ref[...], g_ref[...]
    scale = DH**-0.5
    lane_head = lax.broadcasted_iota(jnp.int32, q.shape, 1) // DH
    key_ok = key_places(k.shape[0], len_ref) < len_ref[1 + pl.program_id(0)]
    grads = [jnp.zeros(q.shape, F32)] * 3
    for h in range(LANES // DH):
        probs = head_probs(q, k, lane_head, h, key_ok, scale)
        g_h = jnp.where(lane_head == h, g, jnp.zeros_like(g))
        grad_probs = dot(g_h, v, 1, 1)
        inner = jnp.sum(probs * grad_probs, axis=-1, keepdims=True)
        grad_scores = (probs * (grad_probs - inner)).astype(BF16)
        mine = lane_head == h
        new = (
            dot(grad_scores, k, 1, 0) * scale,
            dot(grad_scores, q, 0, 0) * scale,
            dot(probs.astype(BF16), g, 0, 0),
        )
        grads = [jnp.where(mine, n, old) for n, old in zip(new, grads)]
    width = d_ref.shape[1] // 3
    for part, grad in enumerate(grads):
        low = grad.astype(BF16)
        start = pl.multiple_of(part * width + pl.program_id(1) * LANES, LANES)
        d_ref[:, pl.ds(start, LANES)] = low
        sum_ref[0, :, pl.ds(start, LANES)] = jnp.sum(low.astype(F32), axis=0, keepdims=True)


def qkv_specs(full_len, pairs):
    return [
        pl.BlockSpec((full_len, LANES), functools.partial(lambda s, j, n, off: (s, j + off), off=pairs * i))
        for i in range(3)
    ]


def attend(slot_lengths, mixed, full_len):
    slots, width = slot_lengths.shape[0] - 1, mixed.shape[1] // 3
    pairs = width // LANES
    return pl.pallas_call(
        attend_body,
        out_shape=jax.ShapeDtypeStruct((mixed.shape[0], width), BF16),
        grid_spec=pltpu.PrefetchScalarGridSpec(
            num_scalar_prefetch=1,
            grid=(slots, pairs),
            in_specs=qkv_specs(full_len, pairs),
            out_specs=pl.BlockSpec((full_len, LANES), lambda s, j, n: (s, j)),
        ),
        name="attend",
    )(slot_lengths, mixed, mixed, mixed)


def attend_back(slot_lengths, mixed, grad_att, full_len):
    slots, width = slot_lengths.shape[0] - 1, mixed.shape[1] // 3
    pairs = width // LANES
    plain = pl.BlockSpec((full_len, LANES), lambda s, j, n: (s, j))
    return pl.pallas_call(
        attend_back_body,
        out_shape=[
            jax.ShapeDtypeStruct(mixed.shape, BF16),
            jax.ShapeDtypeStruct((slots, 1, mixed.shape[1]), F32),
        ],
        grid_spec=pltpu.PrefetchScalarGridSpec(
            num_scalar_prefetch=1,
            grid=(slots, pairs),
            in_specs=qkv_specs(full_len, pairs) + [plain],
            out_specs=[
                pl.BlockSpec((full_len, mixed.shape[1]), lambda s, j, n: (s, 0)),
                pl.BlockSpec((1, 1, mixed.shape[1]), lambda s, j, n: (s, 0, 0)),
            ],
        ),
        name="attend_back",
    )(slot_lengths, mixed, mixed, mixed, grad_att)


def swap_cores(value):
    return lax.ppermute(value, "tp", [(0, 1), (1, 0)])


def swap_ctx(value, bit):
    return lax.ppermute(value, "ctx", [(i, i ^ bit) for i in range(CTX)])


def shift_outer(value, step):
    count = lax.axis_size("fsdp")
    return lax.ppermute(value, "fsdp", [(i, (i + step) % count) for i in range(count)])


class Order:
    def __init__(self):
        self.last = None

    def tie(self, *values):
        if self.last is not None:
            values, _ = lax.optimization_barrier((values, self.last))
        return values

    def run(self, fn, *values):
        out = fn(*self.tie(*values))
        self.last = jax.tree.leaves(out)[0]
        return out

    def arrive(self, *values):
        values = self.tie(*values)
        self.last = values
        return values


BLOCKS = ((0, 0), (0, 1), (1, 0), (1, 2), (0, 2), (0, 3), (1, 1), (1, 3))


def owner_order():
    outer = lax.axis_size("fsdp")
    half = outer // 2
    distance = np.array([d for _, d in BLOCKS for _ in range(half)], np.int32)
    step = np.array([side * half + i for side, _ in BLOCKS for i in range(half)], np.int32)
    place = (lax.axis_index("fsdp") - step) % outer if outer <= DIRECT else jnp.asarray(step)
    return place * CTX + (lax.axis_index("ctx") ^ distance)


def outer_start(shard):
    outer = lax.axis_size("fsdp")
    if outer <= DIRECT:
        return [shard] + [shift_outer(shard, s) for s in range(1, outer)]
    return list(lax.all_gather(shard, "fsdp", axis=0, tiled=False))


def inner_start(order, pieces):
    half = len(pieces) // 2
    a, b = order.run(
        lambda *p: (jnp.concatenate(p[:half], axis=0), jnp.concatenate(p[half:], axis=0)), *pieces
    )
    return dict(
        a0=a, b0=b, a1=swap_ctx(a, 1), b2=swap_ctx(b, 2), b1=swap_ctx(b, 1), a2=swap_ctx(a, 2)
    )


def inner_second(order, got):
    a1, b2 = order.arrive(got["a1"], got["b2"])
    return dict(got, a1=a1, b2=b2, a3=swap_ctx(a1, 2), b3=swap_ctx(b2, 1))


def inner_join(order, got, parts):
    starts = [sum(parts[:i]) for i in range(len(parts))]
    return order.run(
        lambda *p: [
            jnp.concatenate([v[:, s : s + n] for v in p], axis=0) for s, n in zip(starts, parts)
        ],
        *[got["ab"[side] + str(d)] for side, d in BLOCKS],
    )


class Reduction:
    def __init__(self, order, make, rows, *operands):
        self.order, self.make, self.operands = order, make, operands
        self.cut = rows // 8

    def half(self, w):
        return [v[w] if isinstance(v, list) else v for v in self.operands]

    def mates(self):
        cut = self.cut
        for name, span in (("mate_sent", slice(4 * cut, 8 * cut)), ("mate_kept", slice(0, 4 * cut))):
            part = self.order.run(
                lambda *v: self.make(span, 1, *v).astype(BF16), *self.half(1)
            )
            setattr(self, name, swap_cores(part))

    def first(self):
        cut = self.cut
        both = []
        for i in range(2):
            span = slice((4 + 2 * i) * cut, (6 + 2 * i) * cut)
            there = slice(2 * i * cut, (2 * i + 2) * cut)
            both.append(
                self.order.run(
                    lambda m, *v: (self.make(span, 0, *v) + m[there].astype(F32)).astype(BF16),
                    self.mate_sent,
                    *self.half(0),
                )
            )
        self.a, self.b = swap_ctx(both[0], 2), swap_ctx(both[1], 1)

    def keep(self):
        cut = self.cut
        self.kept = self.order.run(
            lambda m, *v: self.make(slice(0, 4 * cut), 0, *v) + m.astype(F32),
            self.mate_kept,
            *self.half(0),
        )

    def second(self):
        cut = self.cut
        a, b = self.order.run(
            lambda k, x, y: (
                (k[cut : 2 * cut] + x[cut:].astype(F32)).astype(BF16),
                (k[3 * cut :] + y[cut:].astype(F32)).astype(BF16),
            ),
            self.kept,
            self.a,
            self.b,
        )
        self.a2, self.b2 = swap_ctx(a, 1), swap_ctx(b, 2)

    def third(self):
        cut = self.cut
        outer = lax.axis_size("fsdp")
        per = 2 * cut // outer

        def add(k, x, y, x2, y2):
            a = k[:cut] + x[:cut].astype(F32) + x2.astype(F32)
            b = k[2 * cut : 3 * cut] + y[:cut].astype(F32) + y2.astype(F32)
            if outer > DIRECT:
                return [jnp.concatenate([a, b], axis=0).astype(BF16)]
            pieces = [v[i * per : (i + 1) * per] for v in (a, b) for i in range(outer // 2)]
            return pieces[:1] + [p.astype(BF16) for p in pieces[1:]]

        pieces = self.order.run(add, self.kept, self.a, self.b, self.a2, self.b2)
        if outer > DIRECT:
            self.pieces = [
                lax.psum_scatter(pieces[0], "fsdp", scatter_dimension=0, tiled=True)
            ]
        else:
            self.pieces = pieces[:1] + [shift_outer(pieces[s], -s) for s in range(1, outer)]

    def result(self):
        return sum(p.astype(F32) for p in self.pieces)


def place_pairs(own, mate, dtype):
    place = jnp.stack([lax.axis_index("tp"), lax.axis_index("ctx")]).astype(jnp.int32)
    _, rows, width = own.shape

    def body(place_ref, own_ref, mate_ref, out_ref):
        for d in range(CTX):
            out_ref[place_ref[0], place_ref[1] ^ d] = own_ref[d].astype(dtype)
            out_ref[1 - place_ref[0], place_ref[1] ^ d] = mate_ref[d].astype(dtype)

    step = 32
    spec = pl.BlockSpec((CTX, step, width), lambda i, p: (0, i, 0))
    return pl.pallas_call(
        body,
        out_shape=jax.ShapeDtypeStruct((2, CTX, rows, width), dtype),
        grid_spec=pltpu.PrefetchScalarGridSpec(
            num_scalar_prefetch=1,
            grid=(rows // step,),
            in_specs=[spec, spec],
            out_specs=pl.BlockSpec((2, CTX, step, width), lambda i, p: (0, 0, i, 0)),
        ),
        name="place_pairs",
    )(place, own, mate)


def normalize(values, norm_gain, norm_shift):
    center = values - jnp.mean(values, axis=-1, keepdims=True)
    inverse = lax.rsqrt(jnp.mean(center * center, axis=-1, keepdims=True) + EPSILON)
    unit_rows = center * inverse
    return (unit_rows * norm_gain + norm_shift, unit_rows, inverse)


def normalize_back(incoming, unit_rows, inverse, norm_gain):
    scaled = incoming * norm_gain
    inner = jnp.mean(scaled * unit_rows, axis=-1, keepdims=True)
    result = inverse * (scaled - jnp.mean(scaled, axis=-1, keepdims=True) - unit_rows * inner)
    return (result, jnp.sum(incoming * unit_rows, axis=0), jnp.sum(incoming, axis=0))


def gelu_parts(upward):
    cdf = 0.5 * (1.0 + lax.erf(upward * ROOT_HALF))
    slope = cdf + upward * INV_ROOT_TAU * jnp.exp(-0.5 * upward * upward)
    return (upward * cdf).astype(BF16), slope


def pack_rows(vectors, q_bias, v_bias, up_bias, rows):
    per = vectors[0].shape[-1]
    lines = [jnp.pad(v, ((0, 0), (0, LANES - per))) for v in vectors]
    mixed = jnp.concatenate([q_bias, v_bias], axis=-1)
    lines.append(jnp.pad(mixed, ((0, 0), (0, LANES - mixed.shape[-1]))))
    lines.append(jnp.pad(up_bias, ((0, 0), (0, LANES - up_bias.shape[-1]))))
    packed = jnp.stack(lines, axis=1)
    return jnp.pad(packed, ((0, 0), (0, rows - packed.shape[1]), (0, 0)))


def shards(
    hidden_in,
    lengths,
    cotangent,
    w_qkv,
    q_bias,
    v_bias,
    w_out,
    out_bias,
    norm1_gain,
    norm1_shift,
    w_up,
    up_bias,
    w_down,
    down_bias,
    norm2_gain,
    norm2_shift,
):
    micro_count, seq_count, local_len, width = hidden_in.shape
    ctx_count = lax.axis_size("ctx")
    core_count = lax.axis_size("tp")
    core = lax.axis_index("tp")
    owners = lax.axis_size("fsdp") * ctx_count
    full_len = local_len * ctx_count
    pair_count = micro_count * seq_count
    slots = pair_count // (ctx_count * core_count)
    per_core = pair_count // core_count
    rows = w_qkv.shape[0]
    head_width = w_qkv.shape[2]
    qkv_width = 3 * head_width
    hidden_units = w_up.shape[1]
    q_per, up_per = q_bias.shape[1], up_bias.shape[1]

    order = Order()
    run = order.run
    both = range(2)
    here = lax.axis_index("ctx")
    slot_first = (core * ctx_count + here) * slots
    slot_lengths = lax.dynamic_slice_in_dim(lengths.reshape(pair_count), slot_first, slots, 0)
    slot_table = jnp.concatenate([here.astype(jnp.int32)[None], slot_lengths])
    owner_list = owner_order()
    feature = (owner_list[:, None] * rows + jnp.arange(rows, dtype=jnp.int32)).reshape(1, width)
    move = (lax.broadcasted_iota(jnp.int32, (width, width), 0) == feature).astype(BF16)
    owner_move = (lax.broadcasted_iota(jnp.int32, (owners, owners), 1) == owner_list[:, None]).astype(BF16)

    def send_slots(value):
        value = value.reshape(pair_count, local_len, width)
        parts = [
            lax.dynamic_slice_in_dim(value, core * per_core + (here ^ d) * slots, slots, 0)
            for d in range(ctx_count)
        ]
        return parts[:1] + [swap_ctx(parts[d], d) for d in range(1, ctx_count)]

    def take_slots(*parts):
        value = jnp.stack(parts, axis=1).reshape(slots * full_len, width)
        return dot(value, move, 1, 0).astype(BF16)

    def send_positions(value):
        natural = run(lambda v, m: dot(v, m, 1, 1).astype(BF16), value, move)
        natural = natural.reshape(slots, ctx_count, local_len, width)
        parts = [natural[:, d] for d in range(ctx_count)]
        return parts[:1] + [swap_ctx(parts[d], d) for d in range(1, ctx_count)]

    def take_positions(parts):
        own = run(lambda *p: jnp.stack(p).reshape(ctx_count, slots * local_len, width), *parts)
        return own, swap_cores(own)

    def all_pairs(own, mate, dtype):
        return run(lambda o, m: place_pairs(o, m, dtype), own, mate).reshape(hidden_in.shape)

    small = pack_rows(
        [v[None] for v in (out_bias, norm1_gain, norm1_shift, down_bias, norm2_gain, norm2_shift)],
        q_bias,
        v_bias,
        up_bias,
        rows,
    )[0]
    shard_one = jnp.concatenate([w_qkv.reshape(rows, qkv_width), w_out.T, small], axis=1)
    far_one = outer_start(shard_one)
    in_parts = send_slots(hidden_in)
    cot_parts = send_slots(cotangent)
    got_one = inner_start(order, far_one)
    far_up = outer_start(order.tie(w_up)[0])
    inputs = run(take_slots, *in_parts)
    got_one = inner_second(order, got_one)
    cot_rows = run(take_slots, *cot_parts)
    got_up = inner_start(order, far_up)
    far_down = outer_start(order.tie(w_down)[0].T)
    qkv_own, rest_own = inner_join(order, got_one, (qkv_width, head_width + LANES))
    qkv_w = (qkv_own, swap_cores(qkv_own))
    rest_w = (rest_own, swap_cores(rest_own))
    out_w = [r[:, :head_width] for r in rest_w]
    packs = [r[:, head_width:].reshape(owners, rows, LANES)[:, :8] for r in rest_w]

    def vector(line):
        return packs[0][:, line, :rows].reshape(1, width).astype(F32)

    def natural(line, w, start, size):
        return dot(owner_move, packs[w][:, line, start : start + size], 0, 0).reshape(1, owners * size)

    def mix(w):
        q_part, v_part = natural(6, w, 0, q_per), natural(6, w, q_per, q_per)
        bias = jnp.concatenate([q_part, jnp.zeros((1, head_width), F32), v_part], axis=1)
        return run(lambda x, k: (dot(x, k, 1, 0) + bias).astype(BF16), inputs, qkv_w[w])

    b_out, gain_one, shift_one, b_down, gain_two, shift_two = [vector(i) for i in range(6)]
    mixed, attended = [None, None], [None, None]
    mixed[0] = mix(0)
    attended[0] = run(lambda m: attend(slot_table, m, full_len), mixed[0])
    got_up = inner_second(order, got_up)
    got_down = inner_start(order, far_down)
    mixed[1] = mix(1)
    attended[1] = run(lambda m: attend(slot_table, m, full_len), mixed[1])
    up_own = inner_join(order, got_up, (hidden_units,))[0]
    up_w = (up_own, swap_cores(up_own))
    projected = run(
        lambda a, b: dot(a, out_w[0], 1, 1) + dot(b, out_w[1], 1, 1), attended[0], attended[1]
    )
    normed, unit_one, inverse_one = normalize(
        inputs.astype(F32) + projected + b_out, gain_one, shift_one
    )
    normed_low = run(lambda n: n.astype(BF16), normed)
    got_down = inner_second(order, got_down)
    activated, slope = [], []
    for w in both:
        bias = natural(7, w, 0, up_per)
        act, slp = run(lambda n, k: gelu_parts(dot(n, k, 1, 0) + bias), normed_low, up_w[w])
        activated.append(act)
        slope.append(slp)
    down_own = inner_join(order, got_down, (hidden_units,))[0]
    down_w = (down_own, swap_cores(down_own))
    downward = run(lambda a, k: dot(a, k, 1, 1), activated[0], down_w[0])
    downward = run(lambda a, k, d: d + dot(a, k, 1, 1), activated[1], down_w[1], downward)
    result, unit_two, inverse_two = normalize(normed + downward + b_down, gain_two, shift_two)

    row = lax.broadcasted_iota(jnp.int32, (slots, full_len, 1), 1)
    part = row // local_len
    place = (part ^ here) * local_len + (row - part * local_len)
    valid = (place < slot_lengths[:, None, None]).reshape(slots * full_len, 1)
    masked_cot = cot_rows.astype(F32) * valid.astype(F32)
    grad_two, g_gain_two, g_shift_two = normalize_back(masked_cot, unit_two, inverse_two, gain_two)
    g_down_bias = jnp.sum(grad_two, axis=0)
    grad_two_low, result_low = run(lambda g, r: (g.astype(BF16), r.astype(BF16)), grad_two, result)

    def product(s, w, x, y):
        return dot(x[:, s], y, 0, 0)

    red_down = Reduction(order, product, width, grad_two_low, activated)
    red_down.mates()
    out_parts = send_positions(result_low)
    red_down.first()
    grad_up = [None, None]

    def up_grad(w):
        grad_up[w] = run(
            lambda g, k, s: (dot(g, k, 1, 0) * s).astype(BF16), grad_two_low, down_w[w], slope[w]
        )

    up_grad(1)
    red_up = Reduction(order, product, width, normed_low, grad_up)
    red_up.mates()
    red_down.keep()
    out_own, out_mate = take_positions(out_parts)
    up_grad(0)
    red_down.second()
    red_up.first()
    red_up.keep()
    back_up = run(lambda g, k: dot(g, k, 1, 1), grad_up[0], up_w[0])
    back_up = run(lambda g, k, d: d + dot(g, k, 1, 1), grad_up[1], up_w[1], back_up)
    red_down.third()
    grad_normed = grad_two + back_up
    grad_one, g_gain_one, g_shift_one = normalize_back(grad_normed, unit_one, inverse_one, gain_one)
    g_out_bias = jnp.sum(grad_one, axis=0)
    grad_one_low = run(lambda g: g.astype(BF16), grad_one)
    grad_mixed, d_small = [None, None], [None, None]
    lines = [g_out_bias, g_gain_one, g_shift_one, g_down_bias, g_gain_two, g_shift_two]
    lines = [v.reshape(owners, rows).astype(BF16) for v in lines]

    def back(w):
        grad_att = run(lambda g, k: dot(g, k, 1, 0).astype(BF16), grad_one_low, out_w[w])
        grad_mixed[w], sums = run(
            lambda m, g: attend_back(slot_table, m, g, full_len), mixed[w], grad_att
        )
        sums = jnp.sum(sums, axis=0)[0]
        up_sums = jnp.sum(grad_up[w].astype(F32), axis=0)

        def by_owner(v):
            return dot(owner_move, v.astype(BF16).reshape(owners, -1), 1, 0).astype(BF16)

        d_small[w] = pack_rows(
            lines,
            by_owner(sums[:head_width]),
            by_owner(sums[2 * head_width :]),
            by_owner(up_sums),
            rows,
        ).reshape(width, LANES)

    back(1)
    red_up.second()

    def grad_block(s, w, x, g_mixed, g_one, att, line):
        return jnp.concatenate(
            [dot(x[:, s], g_mixed, 0, 0), dot(g_one[:, s], att, 0, 0), line[s].astype(F32)], axis=1
        )

    red_one = Reduction(
        order, grad_block, width, inputs, grad_mixed, grad_one_low, attended, d_small
    )
    red_one.mates()
    back(0)
    red_up.third()
    red_one.first()
    red_one.keep()
    grad_inputs = run(lambda g, k, d: d + dot(g, k, 1, 1), grad_mixed[0], qkv_w[0], grad_one)
    grad_inputs = run(
        lambda g, k, d: (d + dot(g, k, 1, 1)).astype(BF16), grad_mixed[1], qkv_w[1], grad_inputs
    )
    in_parts = send_positions(grad_inputs)
    output = all_pairs(out_own, out_mate, BF16)
    g_down, g_up = run(lambda *p: (sum(v.astype(F32) for v in p[: len(p) // 2]), sum(v.astype(F32) for v in p[len(p) // 2 :])), *red_down.pieces, *red_up.pieces)
    red_one.second()
    in_own, in_mate = take_positions(in_parts)
    red_one.third()
    input_grad = all_pairs(in_own, in_mate, F32)
    g_one = red_one.result()
    tail = g_one[:8, qkv_width + head_width :]
    return (
        output,
        input_grad,
        g_one[:, :qkv_width].reshape(rows, 3, head_width),
        tail[6:7, :q_per],
        tail[6:7, q_per : 2 * q_per],
        g_one[:, qkv_width : qkv_width + head_width].T,
        tail[0, :rows],
        tail[1, :rows],
        tail[2, :rows],
        g_up,
        tail[7:8, :up_per],
        g_down.T,
        tail[3, :rows],
        tail[4, :rows],
        tail[5, :rows],
    )


def solution(mesh):
    owner = ("fsdp", "ctx")
    tokens = P(None, "fsdp", "ctx", None)
    weights = (
        P(owner, None, "tp"),
        P("tp", owner),
        P("tp", owner),
        P("tp", owner),
        P(owner),
        P(owner),
        P(owner),
        P(owner, "tp"),
        P("tp", owner),
        P("tp", owner),
        P(owner),
        P(owner),
        P(owner),
    )
    return jax.shard_map(
        shards,
        mesh=mesh,
        in_specs=(tokens, P(None, "fsdp"), tokens) + weights,
        out_specs=(tokens, tokens) + weights,
        check_vma=False,
    )
```
